32 devices in a mesh: members: 2 (over y), lat: 4 (over x, core), blk: 4 (over z).
Axes of the slice: x: 2, y: 2, z: 4, core: 2. Of those that a mesh axis runs over, the one named last changes fastest.
Arguments:
- starting_states: float32 [512, 256, 768], P(('members', 'blk'), 'lat'), may hold values from -6 to 6
- courant_x: float32 [256, 768], P('lat'), may hold values from -0.3 to 0.3
- courant_y: float32 [256, 768], P('lat'), may hold values from -0.3 to 0.3
- diffusion: float32 [256, 768], P('lat'), may hold values from 0.05 to 0.2
- obs_index: int32 [4, 8, 128], P('lat', ('members', 'blk')), may hold values from 0 to 6143
- obs_value: float32 [4, 8, 128], P('lat', ('members', 'blk')), may hold values from -6 to 6
- loc_weight: float32 [4, 8, 3, 128], P('lat', ('members', 'blk')), may hold values from 0.1 to 1
Outputs:
- analysis: float32 [512, 256, 768], P(('members', 'blk'), 'lat')
The draws below stay inside these ranges and needn't reach their ends.
Inputs may be any that keep to these rules, and one draw needn't show every extreme that they name: `obs_index`: positions among the 6144 cells of the block, counted row by row; repeats may occur.
All inputs are finite; a program needn't handle non-finite values.
Results may differ from the reference program's by a relative error of at most 0.0003.
Values sent between devices are 32-bit elements; how exact they have to be, the bound alone decides.
No kernel may reach another device: no remote copies, remote signals or barrier semaphores. Data moves between devices by JAX's collectives and lax.ppermute only.
A program may use at most 128 MiB of HBM per device.

```python
import math
import jax
import jax.numpy as jnp
from jax import lax

MEMBERS = 512
NLON = 768
OBS = 128
FSTEPS = 8
NS_ITERS = 4
NLAT = 256
CELLS_BLK = 6144
SUBS = 8
N_LAT = 4


def place_ends(values, stream_key, smallest, top_value):
    index_at = [jax.random.randint(jax.random.fold_in(stream_key, axis), (), 0, length) for axis, length in enumerate(values.shape)]
    widest = values.shape.index(max(values.shape))
    next_to = index_at[:widest] + [(index_at[widest] + 1) % values.shape[widest]] + index_at[widest + 1:]
    return values.at[tuple(index_at)].set(smallest).at[tuple(next_to)].set(top_value)


def steps_of(rng, shape, cuts, smallest, high):
    def one(position, blocks):
        steps = jax.random.uniform(jax.random.fold_in(jax.random.fold_in(rng, 6), position), (blocks,), jnp.float32, smallest / len(cuts), high / len(cuts))
        return jnp.repeat(jnp.exp(steps), shape[position] // blocks).reshape((-1,) + (1,) * (len(shape) - position - 1))

    loudness = one(*cuts[0])
    for cut in cuts[1:]:
        loudness = loudness * one(*cut)
    return loudness


def bell_draw(rng, shape, width, limit, cuts=(), kind=jnp.bfloat16):
    entries = width * jax.random.normal(rng, shape, jnp.float32)
    if cuts:
        entries = entries * steps_of(rng, shape, cuts, -0.22, 0.18)
    return jnp.clip(entries, -limit, limit).astype(kind)


def setup_inputs(seed: int = 0) -> dict:
    splits = jax.random.split(jax.random.key(seed), 8)
    starting_states = bell_draw(splits[0], (MEMBERS, NLAT, NLON), 1.0, 6.0, ((0, 8), (1, 4)), jnp.float32)
    courant_x = jnp.clip(jax.random.uniform(splits[1], (NLAT, NLON), jnp.float32, -0.3, 0.3) * steps_of(splits[1], (NLAT, NLON), ((0, 4),), -0.4, 0.0), -0.3, 0.3)
    courant_y = jnp.clip(jax.random.uniform(splits[2], (NLAT, NLON), jnp.float32, -0.3, 0.3) * steps_of(splits[2], (NLAT, NLON), ((0, 4),), -0.4, 0.0), -0.3, 0.3)
    diffusion = jnp.clip(0.05 + 0.15 * jax.random.uniform(splits[3], (NLAT, NLON), jnp.float32) ** steps_of(splits[3], (NLAT, NLON), ((0, 4),), -0.2, 0.2), 0.05, 0.2)
    obs_index = place_ends(jax.random.randint(splits[4], (N_LAT, SUBS, OBS), 0, CELLS_BLK), jax.random.fold_in(splits[4], 1), 0, CELLS_BLK - 1).astype(jnp.int32)
    obs_value = bell_draw(splits[5], (N_LAT, SUBS, OBS), 1.0, 6.0, ((0, 4), (1, 8)), jnp.float32)
    loc_weight = jnp.clip(jnp.exp(math.log(1.0) - 2.3025851 * jax.random.uniform(splits[6], (N_LAT, SUBS, 3, OBS), jnp.float32) ** steps_of(splits[6], (N_LAT, SUBS, 3, OBS), ((0, 4), (1, 8)), -0.2, 0.2)), 0.1, 1.0)
    return dict(starting_states=starting_states, courant_x=courant_x, courant_y=courant_y, diffusion=diffusion, obs_index=obs_index, obs_value=obs_value, loc_weight=loc_weight)


HIGH = lax.Precision.HIGHEST

def advance(field_now, courant_x, courant_y, diffusion):
    zero_row = jnp.zeros((1, field_now.shape[1]), jnp.float32)
    row_above = jnp.concatenate([field_now[1:], zero_row], axis=0)
    row_below = jnp.concatenate([zero_row, field_now[:-1]], axis=0)
    eastward_column = jnp.roll(field_now, -1, axis=1)
    col_west = jnp.roll(field_now, 1, axis=1)
    return field_now + 0.5 * courant_x * (col_west - eastward_column) + 0.5 * courant_y * (row_below - row_above) + diffusion * (eastward_column + col_west + row_above + row_below - 4.0 * field_now)

def transform(block, stacked_members, innovation, weights):
    realization_number = block.shape[0]
    centre = lax.optimization_barrier(jnp.mean(block, axis=0))
    anomaly = block - centre
    weighted = stacked_members * weights
    identity = jnp.eye(realization_number, dtype=jnp.float32)
    gram = identity + jnp.dot(weighted, stacked_members.T, precision=HIGH) / (realization_number - 1)
    frobenius = jnp.sqrt(jnp.sum(gram * gram) + 1e-06)
    iterate = gram / frobenius
    inverse = identity
    for repeat in range(NS_ITERS):
        factor = 1.5 * identity - 0.5 * jnp.dot(inverse, iterate, precision=HIGH)
        iterate = jnp.dot(iterate, factor, precision=HIGH)
        inverse = jnp.dot(factor, inverse, precision=HIGH)
    inv_root = inverse / jnp.sqrt(frobenius)
    pull_term = jnp.dot(weighted, innovation, precision=HIGH)
    shift_mean = jnp.dot(inv_root, jnp.dot(inv_root, pull_term, precision=HIGH), precision=HIGH) / (realization_number - 1)
    mixing = inv_root + shift_mean[:, None]
    return centre[None, :] + jnp.dot(mixing.T, anomaly, precision=HIGH)

def reference(starting_states, courant_x, courant_y, diffusion, obs_index, obs_value, loc_weight):

    def prognosis_surface(realization_thickness):
        for repeat in range(FSTEPS):
            realization_thickness = advance(realization_thickness, courant_x, courant_y, diffusion)
        return realization_thickness
    projected_thickness = lax.map(prognosis_surface, starting_states)
    block_count = N_LAT * SUBS
    blocks = jnp.transpose(projected_thickness.reshape(MEMBERS, block_count, CELLS_BLK), (1, 0, 2))
    positions = obs_index.reshape(block_count, OBS)
    observed = obs_value.reshape(block_count, OBS)
    weight_rows = loc_weight.reshape(block_count, 3 * OBS)

    def observe(packed_values):
        block, cells, values = packed_values
        ybank = jnp.take(block, cells, axis=1)
        ybar = lax.optimization_barrier(jnp.mean(ybank, axis=0))
        return (ybank - ybar, values - ybar)
    own_anom, local_innovation = lax.map(observe, (blocks, positions, observed))
    strips_anom = own_anom.reshape(N_LAT, SUBS, MEMBERS, OBS)
    strips_innov = local_innovation.reshape(N_LAT, SUBS, OBS)
    zero_anom = jnp.zeros((N_LAT, 1, MEMBERS, OBS), jnp.float32)
    zero_innov = jnp.zeros((N_LAT, 1, OBS), jnp.float32)
    prev_anom = jnp.concatenate([zero_anom, strips_anom[:, :-1]], axis=1).reshape(block_count, MEMBERS, OBS)
    next_anom = jnp.concatenate([strips_anom[:, 1:], zero_anom], axis=1).reshape(block_count, MEMBERS, OBS)
    prev_innov = jnp.concatenate([zero_innov, strips_innov[:, :-1]], axis=1).reshape(block_count, OBS)
    next_innovation = jnp.concatenate([strips_innov[:, 1:], zero_innov], axis=1).reshape(block_count, OBS)

    def analyse(packed_values):
        block, anom_prev, anom_own, anom_next, innov_prev, innov_own, innov_next, weights = packed_values
        stacked_members = jnp.concatenate([anom_prev, anom_own, anom_next], axis=1)
        innovation = jnp.concatenate([innov_prev, innov_own, innov_next], axis=0)
        return transform(block, stacked_members, innovation, weights)
    corrected_states = lax.map(analyse, (blocks, prev_anom, own_anom, next_anom, prev_innov, local_innovation, next_innovation, weight_rows))
    return jnp.transpose(corrected_states, (1, 0, 2)).reshape(MEMBERS, NLAT, NLON)
```

```python
import functools
import jax
import jax.numpy as jnp
from jax import lax
from jax.experimental import pallas as pl
from jax.experimental.pallas import tpu as pltpu
from jax.sharding import PartitionSpec as P


FSTEPS = 8
NS_ITERS = 4
LANES = 128

HIGH = lax.Precision.HIGHEST
GROUP = ("members", "blk")
F32 = jnp.float32
BF16 = jnp.bfloat16


def call(kernel, flops, moved, **kwargs):
    return pl.pallas_call(
        kernel,
        compiler_params=pltpu.CompilerParams(vmem_limit_bytes=48 << 20),
        cost_estimate=pl.CostEstimate(flops=flops, bytes_accessed=moved, transcendentals=0),
        **kwargs,
    )


def shifted(array, axis, by):
    size = lax.axis_size(axis)
    pairs = [(i, i + by) for i in range(size) if 0 <= i + by < size]
    return lax.ppermute(array, axis, pairs)


def forecast_body(unroll, x_ref, low_ref, high_ref, coeff_ref, y_ref, even_ref, odd_ref):
    rows, _, lon = y_ref.shape
    halo = FSTEPS
    total = rows + 2 * halo
    even_ref[0:halo] = jnp.swapaxes(low_ref[...], 0, 1)
    even_ref[halo + rows :] = jnp.swapaxes(high_ref[...], 0, 1)
    for first in range(0, rows, 8):
        even_ref[halo + first : halo + first + 8] = jnp.swapaxes(
            x_ref[:, first : first + 8, :], 0, 1
        )
    src, dst = even_ref, odd_ref
    for step in range(FSTEPS):
        first, last = step + 1, total - 1 - step

        def advance(row, src=src, dst=dst, final=step == FSTEPS - 1):
            here = src[row]
            east = pltpu.roll(here, lon - 1, 1)
            west = pltpu.roll(here, 1, 1)
            c = [coeff_ref[k, pl.ds(row, 1), :] for k in range(5)]
            new = c[0] * here + c[1] * west + c[2] * east + c[3] * src[row - 1] + c[4] * src[row + 1]
            if final:
                y_ref[row - halo] = new
            else:
                dst[row] = new

        def several(i, carry, first=first, advance=advance):
            for k in range(unroll):
                advance(first + i * unroll + k)
            return carry

        trips = (last - first) // unroll
        lax.fori_loop(0, trips, several, 0)
        for row in range(first + trips * unroll, last):
            advance(row)
        src, dst = dst, src


def forecast(x, low, high, coeffs, start, halo_start, count):
    _, rows, lon = x.shape
    group = 16 if count % 16 == 0 and start % 16 == 0 and halo_start % 16 == 0 else 8
    total = coeffs.shape[1]
    return call(
        functools.partial(forecast_body, 8),
        flops=9 * FSTEPS * total * count * lon,
        moved=8 * count * rows * lon,
        grid=(count // group,),
        in_specs=[
            pl.BlockSpec((group, rows, lon), lambda i: (start // group + i, 0, 0)),
            pl.BlockSpec((group, FSTEPS, lon), lambda i: (halo_start // group + i, 0, 0)),
            pl.BlockSpec((group, FSTEPS, lon), lambda i: (halo_start // group + i, 0, 0)),
            pl.BlockSpec((5, total, lon), lambda i: (0, 0, 0)),
        ],
        out_specs=pl.BlockSpec((rows, group, lon), lambda i: (0, i, 0)),
        out_shape=jax.ShapeDtypeStruct((rows, count, lon), F32),
        scratch_shapes=[pltpu.VMEM((total, group, lon), F32)] * 2,
    )(x, low, high, coeffs)


def split3(value):
    top = value.astype(BF16)
    rest = value - top.astype(F32)
    middle = rest.astype(BF16)
    return top, middle, (rest - middle.astype(F32)).astype(BF16)


def observe_body(cells_ref, *refs):
    chunks, out_ref = refs[:-1], refs[-1]
    block_rows, _, lon = chunks[0].shape
    obs = cells_ref.shape[-1]
    count = out_ref.shape[1]
    total = jnp.zeros((3 * count, obs), F32)
    place = lax.broadcasted_iota(jnp.int32, (lon, obs), 0)
    for row in range(block_rows):
        field = jnp.concatenate([ref[row] for ref in chunks], axis=0)
        chosen = jnp.where(place + row * lon == cells_ref[0], 1.0, 0.0).astype(BF16)
        total += jnp.dot(
            jnp.concatenate(split3(field), axis=0), chosen, preferred_element_type=F32
        )
    out_ref[0] = total[:count] + total[count : 2 * count] + total[2 * count :]


def observe(chunks, cells):
    rows, _, lon = chunks[0].shape
    blocks, _, obs = cells.shape
    block_rows = rows // blocks
    count = sum(chunk.shape[1] for chunk in chunks)
    return call(
        observe_body,
        flops=6 * count * rows * lon * obs,
        moved=4 * count * rows * lon,
        grid=(blocks,),
        in_specs=[pl.BlockSpec((1, 1, obs), lambda k: (k, 0, 0))]
        + [
            pl.BlockSpec((block_rows, chunk.shape[1], lon), lambda k: (k, 0, 0)) for chunk in chunks
        ],
        out_specs=pl.BlockSpec((1, count, obs), lambda k: (k, 0, 0)),
        out_shape=jax.ShapeDtypeStruct((blocks, count, obs), F32),
    )(cells, *chunks)


def mixing_body(layout, banks_ref, values_ref, weights_ref, mix_high_ref, mix_low_ref):
    sources, _, wide = banks_ref.shape
    size = mix_high_ref.shape[0]
    pieces = []
    for start, count in layout:
        for source in range(sources):
            pieces.append(banks_ref[source, start : start + count, :])
    bank = jnp.concatenate(pieces, axis=0)
    mean = jnp.sum(bank, axis=0, keepdims=True) / size
    stacked = bank - mean
    innovation = values_ref[...] - mean
    weighted = stacked * weights_ref[...]

    def dot(a, b, contract=((1,), (0,))):
        return lax.dot_general(a, b, (contract, ((), ())), precision=HIGH, preferred_element_type=F32)

    shape = (size, size)
    identity = jnp.where(
        lax.broadcasted_iota(jnp.int32, shape, 0) == lax.broadcasted_iota(jnp.int32, shape, 1), 1.0, 0.0
    )
    gram = identity + dot(weighted, stacked, ((1,), (1,))) / (size - 1)
    squares = jnp.sum(jnp.sum(gram * gram, axis=0, keepdims=True), axis=1, keepdims=True)
    frobenius = jnp.sqrt(squares + 1e-06)
    iterate = gram / frobenius
    inverse = 1.5 * identity - 0.5 * iterate
    iterate = dot(iterate, inverse)
    for repeat in range(1, NS_ITERS):
        factor = 1.5 * identity - 0.5 * dot(inverse, iterate)
        if repeat < NS_ITERS - 1:
            iterate = dot(iterate, factor)
        inverse = dot(factor, inverse)
    inv_root = inverse / jnp.sqrt(frobenius)
    wide_row = jnp.broadcast_to(innovation, (8, wide))
    pull = dot(wide_row, weighted, ((1,), (1,)))
    shift = (dot(dot(pull, inv_root), inv_root) / (size - 1))[:1]
    mixing = inv_root + shift
    mixing = mixing + (1.0 - jnp.sum(mixing, axis=1, keepdims=True)) / size
    top = mixing.astype(BF16)
    mix_high_ref[...] = top
    mix_low_ref[...] = (mixing - top.astype(F32)).astype(BF16)


def mixing_matrix(banks, values, weights, layout):
    sources, count, wide = banks.shape
    size = sources * count
    out = jax.ShapeDtypeStruct((size, size), BF16)
    return call(
        functools.partial(mixing_body, layout),
        flops=6 * 2 * 10 * size * size * size,
        moved=4 * size * (wide + size),
        out_shape=(out, out),
    )(banks, values, weights)


def analyse_body(layout, mix_high_ref, mix_low_ref, *refs):
    chunks, out_ref = refs[:-1], refs[-1]
    lanes = out_ref.shape[-1]
    field = jnp.concatenate(
        [ref[:, 0].reshape(ref.shape[0] * ref.shape[2], lanes) for ref in chunks], axis=0
    )
    top = field.astype(BF16)
    low = (field - top.astype(F32)).astype(BF16)

    def dot(a, b):
        return jnp.dot(a, b, preferred_element_type=F32)

    mix_high = mix_high_ref[...]
    result = dot(mix_high, top) + (dot(mix_high, low) + dot(mix_low_ref[...], top))
    at = 0
    targets = out_ref.shape[0]
    for start, count in layout:
        for target in range(targets):
            out_ref[target, 0, start : start + count, :] = result[at : at + count]
            at += count


def analyse(mix_high, mix_low, chunks, layout, first, lanes):
    sources, block_rows, _, _ = chunks[0].shape
    count = sum(chunk.shape[2] for chunk in chunks)
    size = sources * count
    return call(
        functools.partial(analyse_body, layout),
        flops=6 * size * size * block_rows * lanes,
        moved=8 * size * block_rows * lanes,
        grid=(block_rows,),
        in_specs=[pl.BlockSpec((size, size), lambda r: (0, 0))] * 2
        + [
            pl.BlockSpec((sources, 1, chunk.shape[2], lanes), lambda r: (0, r, 0, first // lanes))
            for chunk in chunks
        ],
        out_specs=pl.BlockSpec((sources, 1, count, lanes), lambda r: (0, r, 0, 0)),
        out_shape=jax.ShapeDtypeStruct((sources, block_rows, count, lanes), F32),
    )(mix_high, mix_low, *chunks)


def place_body(part_ref, *refs):
    out_ref = refs[-1]
    rows = out_ref.shape[1]
    for first in range(0, rows, 8):
        out_ref[:, first : first + 8, :] = jnp.swapaxes(part_ref[first : first + 8], 0, 1)


def place(part, whole, first, lon):
    rows, count, lanes = part.shape
    group = 16 if count % 16 == 0 else 8
    out = jax.ShapeDtypeStruct((count, rows, lon), F32)
    return call(
        place_body,
        flops=0,
        moved=8 * rows * count * lanes,
        grid=(count // group,),
        in_specs=[pl.BlockSpec((rows, group, lanes), lambda i: (0, i, 0))]
        + ([] if whole is None else [pl.BlockSpec(memory_space=pl.ANY)]),
        out_specs=pl.BlockSpec((group, rows, lanes), lambda i: (i, 0, first // lanes)),
        out_shape=out,
        input_output_aliases={} if whole is None else {1: 0},
    )(*((part,) if whole is None else (part, whole)))


def member_chunks(count):
    if count == 64:
        return (8, 8, 16, 32)
    return (count,)


def lane_chunks(lon):
    tiles = lon // LANES
    if tiles == 6:
        return (256, 256, 128, 128)
    return (lon,)


def exchange(array):
    return lax.all_to_all(array, GROUP, split_axis=0, concat_axis=0, tiled=True)


def on_device(starting_states, courant_x, courant_y, diffusion, obs_index, obs_value, loc_weight):
    members, rows, lon = starting_states.shape
    blocks = lax.axis_size("members") * lax.axis_size("blk")
    block_rows = rows // blocks
    obs = obs_index.shape[-1]
    counts = member_chunks(members)
    starts = [sum(counts[:i]) for i in range(len(counts))]
    layout = tuple(zip(starts, counts))
    halo = FSTEPS

    def edges(states):
        return shifted(states[:, rows - halo :], "lat", 1), shifted(states[:, :halo], "lat", -1)

    fields = jnp.stack([courant_x, courant_y, diffusion])
    head = sum(counts[:2])
    ends = jnp.concatenate([starting_states[:head, rows - halo :], fields[:, rows - halo :]])
    low = shifted(ends, "lat", 1)
    ends = jnp.concatenate([starting_states[:head, :halo], fields[:, :halo]])
    high = shifted(ends, "lat", -1)
    fields = jnp.concatenate([low[head:], fields, high[head:]], axis=1)
    across, along, spread = 0.5 * fields[0], 0.5 * fields[1], fields[2]
    coeffs = jnp.stack(
        [1.0 - 4.0 * spread, across + spread, spread - across, along + spread, spread - along]
    )

    states, received = [], []
    halos = low[:head], high[:head]
    for i, (start, count) in enumerate(layout):
        early = start < head
        state = forecast(
            starting_states, *halos, coeffs, start, start - (0 if early else head), count
        )
        states.append(state)
        if i == 0 and head < members:
            later, state = lax.optimization_barrier((starting_states, state))
            halos_rest = edges(later[head:])
        if i == 1:
            halos = halos_rest
    local = jnp.concatenate([obs_index.reshape(1, obs).astype(F32), obs_value.reshape(1, obs)])
    local, _ = lax.optimization_barrier((local, states[-1]))
    everyone = lax.all_gather(local[None], GROUP, axis=0, tiled=True)
    for state in states[:-1]:
        received.append(exchange(state.reshape(blocks, block_rows, -1, lon)))

    cells = everyone[:, :1].astype(jnp.int32)
    own = observe(states, cells)
    zero = jnp.zeros((1,) + own.shape[1:], F32)
    triple = jnp.concatenate(
        [jnp.concatenate([zero, own[:-1]]), own, jnp.concatenate([own[1:], zero])], axis=2
    )
    banks = exchange(triple)
    received.append(exchange(states[-1].reshape(blocks, block_rows, -1, lon)))

    zero = jnp.zeros((1, obs), F32)
    values = jnp.concatenate([zero, everyone[:, 1], zero])
    values = lax.dynamic_slice_in_dim(values, lax.axis_index(GROUP), 3).reshape(1, 3 * obs)
    mix_high, mix_low = mixing_matrix(banks, values, loc_weight.reshape(1, 3 * obs), layout)

    result, first = None, 0
    for lanes in lane_chunks(lon):
        part = analyse(mix_high, mix_low, received, layout, first, lanes)
        part = exchange(part)
        result = place(part.reshape(rows, members, lanes), result, first, lon)
        first += lanes
    return result


def solution(mesh):
    in_specs = (
        P(GROUP, "lat", None),
        P("lat", None),
        P("lat", None),
        P("lat", None),
        P("lat", GROUP, None),
        P("lat", GROUP, None),
        P("lat", GROUP, None, None),
    )

    return jax.shard_map(
        on_device, mesh=mesh, in_specs=in_specs, out_specs=P(GROUP, "lat", None), check_vma=False
    )
```

```python
import functools
import jax
import jax.numpy as jnp
from jax import lax
from jax.experimental import pallas as pl
from jax.experimental.pallas import tpu as pltpu
from jax.sharding import PartitionSpec as P


FSTEPS = 8
NS_ITERS = 4
LANES = 128

HIGH = lax.Precision.HIGHEST
GROUP = ("members", "blk")
F32 = jnp.float32
BF16 = jnp.bfloat16


def call(kernel, flops, moved, **kwargs):
    return pl.pallas_call(
        kernel,
        compiler_params=pltpu.CompilerParams(vmem_limit_bytes=48 << 20),
        cost_estimate=pl.CostEstimate(flops=flops, bytes_accessed=moved, transcendentals=0),
        **kwargs,
    )


def shifted(array, axis, by):
    size = lax.axis_size(axis)
    pairs = [(i, i + by) for i in range(size) if 0 <= i + by < size]
    return lax.ppermute(array, axis, pairs)


UNROLL = 16


def forecast_body(x_ref, low_ref, high_ref, coeff_ref, *refs):
    outs, (even_ref, odd_ref) = refs[:-2], refs[-2:]
    _, rows, lon = x_ref.shape
    halo = FSTEPS
    even_ref[0:halo] = jnp.swapaxes(low_ref[...], 0, 1)
    even_ref[halo + rows : 2 * halo + rows] = jnp.swapaxes(high_ref[...], 0, 1)
    for first in range(0, rows, 8):
        even_ref[halo + first : halo + first + 8] = jnp.swapaxes(
            x_ref[:, first : first + 8, :], 0, 1
        )

    def advance(src, dst, first, count):
        def several(i, carry):
            for k in range(UNROLL):
                row = first + i * UNROLL + k
                here = src[row]
                east = pltpu.roll(here, lon - 1, 1)
                west = pltpu.roll(here, 1, 1)
                c = [coeff_ref[k, pl.ds(row, 1), :] for k in range(5)]
                dst[row] = (
                    c[0] * here + c[1] * west + c[2] * east + c[3] * src[row - 1] + c[4] * src[row + 1]
                )
            return carry

        lax.fori_loop(0, (count + UNROLL - 1) // UNROLL, several, 0)

    def two(k, carry):
        first = 2 * k + 1
        count = rows + 2 * halo - 2 * first
        advance(even_ref, odd_ref, first, count)
        advance(odd_ref, even_ref, first + 1, count - 2)
        return carry

    lax.fori_loop(0, FSTEPS // 2, two, 0)
    at = 0
    for out_ref in outs:
        lanes = out_ref.shape[-1]
        out_ref[...] = even_ref[halo : halo + rows, :, at : at + lanes]
        at += lanes


def forecast(x, low, high, coeffs, start, halo_start, count, widths):
    _, rows, lon = x.shape
    group = 16 if count % 16 == 0 and start % 16 == 0 and halo_start % 16 == 0 else 8
    total = coeffs.shape[1]
    return call(
        forecast_body,
        flops=9 * FSTEPS * total * count * lon,
        moved=8 * count * rows * lon,
        grid=(count // group,),
        in_specs=[
            pl.BlockSpec((group, rows, lon), lambda i: (start // group + i, 0, 0)),
            pl.BlockSpec((group, FSTEPS, lon), lambda i: (halo_start // group + i, 0, 0)),
            pl.BlockSpec((group, FSTEPS, lon), lambda i: (halo_start // group + i, 0, 0)),
            pl.BlockSpec((5, total, lon), lambda i: (0, 0, 0)),
        ],
        out_specs=[pl.BlockSpec((rows, group, lanes), lambda i: (0, i, 0)) for lanes in widths],
        out_shape=[pltpu.HBM((rows, count, lanes), F32) for lanes in widths],
        scratch_shapes=[pltpu.VMEM((total, group, lon), F32)] * 2,
    )(x, low, high, coeffs)


def split3(value):
    top = value.astype(BF16)
    rest = value - top.astype(F32)
    middle = rest.astype(BF16)
    return top, middle, (rest - middle.astype(F32)).astype(BF16)


def observe_body(parts, cells_ref, *refs):
    chunks, out_ref = list(refs[:-1]), refs[-1]
    block_rows = chunks[0].shape[0]
    chunks = [[chunks.pop(0) for _ in range(n)] for n in parts]
    lon = sum(ref.shape[-1] for ref in chunks[0])
    obs = cells_ref.shape[-1]
    count = out_ref.shape[1]
    total = jnp.zeros((3 * count, obs), F32)
    place = lax.broadcasted_iota(jnp.int32, (lon, obs), 0)
    for row in range(block_rows):
        field = jnp.concatenate(
            [jnp.concatenate([ref[row] for ref in refs], axis=1) for refs in chunks], axis=0
        )
        chosen = jnp.where(place + row * lon == cells_ref[0], 1.0, 0.0).astype(BF16)
        total += jnp.dot(
            jnp.concatenate(split3(field), axis=0), chosen, preferred_element_type=F32
        )
    out_ref[0] = total[:count] + total[count : 2 * count] + total[2 * count :]


def observe(chunks, cells):
    rows = chunks[0][0].shape[0]
    lon = sum(part.shape[-1] for part in chunks[0])
    blocks, _, obs = cells.shape
    block_rows = rows // blocks
    count = sum(chunk[0].shape[1] for chunk in chunks)
    flat = [part for chunk in chunks for part in chunk]
    return call(
        functools.partial(observe_body, tuple(len(chunk) for chunk in chunks)),
        flops=6 * count * rows * lon * obs,
        moved=4 * count * rows * lon,
        grid=(blocks,),
        in_specs=[pl.BlockSpec((1, 1, obs), lambda k: (k, 0, 0))]
        + [pl.BlockSpec((block_rows,) + part.shape[1:], lambda k: (k, 0, 0)) for part in flat],
        out_specs=pl.BlockSpec((1, count, obs), lambda k: (k, 0, 0)),
        out_shape=jax.ShapeDtypeStruct((blocks, count, obs), F32),
    )(cells, *flat)


def mixing_body(layout, banks_ref, values_ref, weights_ref, top_ref, low_ref, *scratch):
    stacked_ref, weighted_ref, one_ref, two_ref, factor_ref, inverse_ref = scratch
    sources = banks_ref.shape[0]
    size, wide = stacked_ref.shape
    at, start = 0, 0
    for _, count in layout:
        for source in range(sources):
            stacked_ref[at : at + count] = banks_ref[source, start : start + count, :]
            at += count
        start += count
    bank = stacked_ref[...]
    mean = jnp.sum(bank, axis=0, keepdims=True) / size
    stacked = bank - mean
    innovation = values_ref[...] - mean
    weighted = stacked * weights_ref[...]
    stacked_ref[...] = stacked
    weighted_ref[...] = weighted

    def dot(a, b, contract=((1,), (0,))):
        return lax.dot_general(a, b, (contract, ((), ())), precision=HIGH, preferred_element_type=F32)

    strip = size // 2

    def halves(value):
        top = value.astype(BF16)
        return top, (value - top.astype(F32)).astype(BF16)

    def product(dst, a, b, finish=None, contract=((1,), (0,))):
        def rows_of(i, carry):
            rows = pl.ds(pl.multiple_of(i * strip, strip), strip)
            (a_top, a_low), (b_top, b_low) = halves(a[rows, :]), halves(b[...])

            def part(x, y):
                return lax.dot_general(x, y, (contract, ((), ())), preferred_element_type=F32)

            value = part(a_top, b_top) + (part(a_top, b_low) + part(a_low, b_top))
            dst[rows, :] = value if finish is None else finish(i, value)
            return carry

        lax.fori_loop(0, size // strip, rows_of, 0)

    def unit(i, shape):
        row = lax.broadcasted_iota(jnp.int32, shape, 0) + i * strip
        return jnp.where(row == lax.broadcasted_iota(jnp.int32, shape, 1), 1.0, 0.0)

    product(
        one_ref,
        weighted_ref,
        stacked_ref,
        lambda i, value: unit(i, value.shape) + value / (size - 1),
        ((1,), (1,)),
    )
    gram = one_ref[...]
    squares = jnp.sum(jnp.sum(gram * gram, axis=0, keepdims=True), axis=1, keepdims=True)
    frobenius = jnp.sqrt(squares + 1e-06)
    iterate = gram / frobenius
    one_ref[...] = iterate
    inverse_ref[...] = 1.5 * unit(0, iterate.shape) - 0.5 * iterate
    product(two_ref, one_ref, inverse_ref)
    held, spare, inverse = two_ref, one_ref, inverse_ref
    for repeat in range(1, NS_ITERS):
        product(
            factor_ref, inverse, held, lambda i, value: 1.5 * unit(i, value.shape) - 0.5 * value
        )
        if repeat < NS_ITERS - 1:
            product(spare, held, factor_ref)
            held, spare = spare, held
        product(spare, factor_ref, inverse)
        inverse, spare = spare, inverse
    inv_root = inverse[...] / jnp.sqrt(frobenius)
    spare[...] = inv_root
    innovation = jnp.broadcast_to(innovation, (8, wide))
    pull = dot(innovation, weighted_ref[...], ((1,), (1,)))
    shift = (dot(dot(pull, inv_root), inv_root) / (size - 1))[:1]
    mixing = inv_root + shift
    mixing = mixing + (1.0 - jnp.sum(mixing, axis=1, keepdims=True)) / size
    top = mixing.astype(BF16)
    top_ref[...] = top
    low_ref[...] = (mixing - top.astype(F32)).astype(BF16)


def mixing_matrix(banks, values, weights, layout):
    sources, count, wide = banks.shape
    size = sources * count
    out = jax.ShapeDtypeStruct((size, size), BF16)
    return call(
        functools.partial(mixing_body, layout),
        flops=6 * 2 * 10 * size * size * size,
        moved=4 * size * (wide + size),
        out_shape=(out, out),
        scratch_shapes=[pltpu.VMEM((size, wide), F32)] * 2 + [pltpu.VMEM((size, size), F32)] * 4,
    )(banks, values, weights)


def analyse_body(layout, mix_top_ref, mix_low_ref, *refs):
    chunks, out_ref = refs[:-1], refs[-1]
    targets, rows, _, lanes = out_ref.shape
    field = jnp.concatenate(
        [
            jnp.concatenate(
                [ref[:, row].reshape(ref.shape[0] * ref.shape[2], lanes) for row in range(rows)], axis=1
            )
            for ref in chunks
        ],
        axis=0,
    )
    top = field.astype(BF16)
    low = (field - top.astype(F32)).astype(BF16)

    def dot(a, b):
        return jnp.dot(a, b, preferred_element_type=F32)

    mix_top = mix_top_ref[...]
    result = dot(mix_top, top) + (dot(mix_top, low) + dot(mix_low_ref[...], top))
    at = 0
    for start, count in layout:
        for target in range(targets):
            for row in range(rows):
                out_ref[target, row, start : start + count, :] = result[
                    at : at + count, row * lanes : (row + 1) * lanes
                ]
            at += count


def analyse(mix_top, mix_low, chunks, layout, lanes):
    sources, block_rows, _, _ = chunks[0][0].shape
    count = sum(chunk.shape[2] for chunk, _ in chunks)
    size = sources * count
    step = 2 if block_rows % 2 == 0 else 1

    def spec(chunk, first):
        return pl.BlockSpec(
            (sources, step, chunk.shape[2], lanes), lambda r: (0, r, 0, first // lanes)
        )

    return call(
        functools.partial(analyse_body, layout),
        flops=6 * size * size * block_rows * lanes,
        moved=8 * size * block_rows * lanes,
        grid=(block_rows // step,),
        in_specs=[pl.BlockSpec((size, size), lambda r: (0, 0))] * 2
        + [spec(chunk, first) for chunk, first in chunks],
        out_specs=pl.BlockSpec((sources, step, count, lanes), lambda r: (0, r, 0, 0)),
        out_shape=pltpu.HBM((sources, block_rows, count, lanes), F32),
    )(mix_top, mix_low, *[chunk for chunk, _ in chunks])


def place_body(part_ref, *refs):
    out_ref = refs[-1]
    rows = out_ref.shape[1]
    for first in range(0, rows, 8):
        out_ref[:, first : first + 8, :] = jnp.swapaxes(part_ref[first : first + 8], 0, 1)


def place(part, whole, first, lon):
    rows, count, lanes = part.shape
    group = 16 if count % 16 == 0 else 8
    out = jax.ShapeDtypeStruct((count, rows, lon), F32)
    return call(
        place_body,
        flops=0,
        moved=8 * rows * count * lanes,
        grid=(count // group,),
        in_specs=[pl.BlockSpec((rows, group, lanes), lambda i: (0, i, 0))]
        + ([] if whole is None else [pl.BlockSpec(memory_space=pl.ANY)]),
        out_specs=pl.BlockSpec((group, rows, lanes), lambda i: (i, 0, first // lanes)),
        out_shape=out,
        input_output_aliases={} if whole is None else {1: 0},
    )(*((part,) if whole is None else (part, whole)))


def member_chunks(count):
    if count > 24 and count % 16 == 0:
        return (count - 8, 8), (0, 16), (16, count - 24)
    return ((0, count),)


def lane_parts(lon):
    third = lon // 3
    return (2 * third, third) if lon % (3 * LANES) == 0 else (lon,)


def gathered(row):
    size, me = lax.axis_size("members") * lax.axis_size("blk"), lax.axis_index(GROUP)
    bit = 1
    while bit < size:
        other = lax.ppermute(row, GROUP, [(i, i ^ bit) for i in range(size)])
        row = jnp.where(
            (me & bit) == 0, jnp.concatenate([row, other]), jnp.concatenate([other, row])
        )
        bit *= 2
    return row


def exchange(array):
    return lax.all_to_all(array, GROUP, split_axis=0, concat_axis=0, tiled=True)


def exchange_by_steps(array):
    size, me = array.shape[0], lax.axis_index(GROUP)
    if size > 8 or size & (size - 1):
        return exchange(array)
    pieces = [lax.dynamic_slice_in_dim(array, me, 1)]
    for step in range(1, size):
        piece = lax.dynamic_slice_in_dim(array, me ^ step, 1)
        pieces.append(lax.ppermute(piece, GROUP, [(i, i ^ step) for i in range(size)]))
    pieces = jnp.concatenate(pieces)
    return jnp.concatenate([lax.dynamic_slice_in_dim(pieces, me ^ i, 1) for i in range(size)])


def on_device(starting_states, courant_x, courant_y, diffusion, obs_index, obs_value, loc_weight):
    members, rows, lon = starting_states.shape
    blocks = lax.axis_size("members") * lax.axis_size("blk")
    block_rows = rows // blocks
    obs = obs_index.shape[-1]
    layout = member_chunks(members)
    widths = lane_parts(lon)
    halo = FSTEPS

    def edges(states):
        return shifted(states[:, rows - halo :], "lat", 1), shifted(states[:, :halo], "lat", -1)

    fields = jnp.stack([courant_x, courant_y, diffusion])
    early = layout[:2]
    head = sum(count for _, count in early)

    def ends(first):
        return jnp.concatenate(
            [starting_states[at : at + count, first : first + halo] for at, count in early]
            + [fields[:, first : first + halo]]
        )

    low = shifted(ends(rows - halo), "lat", 1)
    high = shifted(ends(0), "lat", -1)
    local = jnp.concatenate([obs_index.reshape(1, obs).astype(F32), obs_value.reshape(1, obs)])
    everyone = gathered(local[None])
    spare = jnp.zeros((3, UNROLL + 8, lon), F32)
    fields = jnp.concatenate([low[head:], fields, high[head:], spare], axis=1)
    across, along, spread = 0.5 * fields[0], 0.5 * fields[1], fields[2]
    coeffs = jnp.stack(
        [1.0 - 4.0 * spread, across + spread, spread - across, along + spread, spread - along]
    )

    states = []
    halos, at = (low[:head], high[:head]), 0
    for i, (start, count) in enumerate(layout):
        parts = widths if i == len(layout) - 1 else (lon,)
        if i == 2:
            halos, at = halos_rest, 0
        state = forecast(starting_states, *halos, coeffs, start, at, count, parts)
        at += count
        states.append(state)
        if i == 0 and len(layout) > 2:
            later, _ = lax.optimization_barrier((starting_states, state[0]))
            halos_rest = edges(later[layout[2][0] : layout[2][0] + layout[2][1]])
    received = []
    for i, state in enumerate(states):
        received.append([])
        for part in state:
            received[i].append(exchange(part.reshape(blocks, block_rows, *part.shape[1:])))

    cells = everyone[:, :1].astype(jnp.int32)
    own = observe(states, cells)
    zero = jnp.zeros((1,) + own.shape[1:], F32)
    triple = jnp.concatenate(
        [jnp.concatenate([zero, own[:-1]]), own, jnp.concatenate([own[1:], zero])], axis=2
    )
    banks = exchange_by_steps(triple)
    zero = jnp.zeros((1, obs), F32)
    values = jnp.concatenate([zero, everyone[:, 1], zero])
    values = lax.dynamic_slice_in_dim(values, lax.axis_index(GROUP), 3).reshape(1, 3 * obs)
    mix_top, mix_low = mixing_matrix(banks, values, loc_weight.reshape(1, 3 * obs), layout)

    result, first = None, 0
    for j, lanes in enumerate(widths):
        chunks = [(chunk[0], first) if len(chunk) == 1 else (chunk[j], 0) for chunk in received]
        part = analyse(mix_top, mix_low, chunks, layout, lanes)
        part = exchange(part)
        result = place(part.reshape(rows, members, lanes), result, first, lon)
        first += lanes
    return result


def solution(mesh):
    in_specs = (
        P(GROUP, "lat", None),
        P("lat", None),
        P("lat", None),
        P("lat", None),
        P("lat", GROUP, None),
        P("lat", GROUP, None),
        P("lat", GROUP, None, None),
    )

    return jax.shard_map(
        on_device, mesh=mesh, in_specs=in_specs, out_specs=P(GROUP, "lat", None), check_vma=False
    )
```

```python
import functools
import jax
import jax.numpy as jnp
from jax import lax
from jax.experimental import pallas as pl
from jax.experimental.pallas import tpu as pltpu
from jax.sharding import PartitionSpec as P


FSTEPS = 8
NS_ITERS = 4
LANES = 128

HIGH = lax.Precision.HIGHEST
GROUP = ("members", "blk")
F32 = jnp.float32
BF16 = jnp.bfloat16


def call(kernel, flops, moved, **kwargs):
    return pl.pallas_call(
        kernel,
        compiler_params=pltpu.CompilerParams(vmem_limit_bytes=48 << 20),
        cost_estimate=pl.CostEstimate(flops=flops, bytes_accessed=moved, transcendentals=0),
        **kwargs,
    )


def shifted(array, axis, by):
    size = lax.axis_size(axis)
    pairs = [(i, i + by) for i in range(size) if 0 <= i + by < size]
    return lax.ppermute(array, axis, pairs)


UNROLL = 16


def forecast_body(x_ref, low_ref, high_ref, coeff_ref, *refs):
    outs, (even_ref, odd_ref) = refs[:-2], refs[-2:]
    _, rows, lon = x_ref.shape
    halo = FSTEPS
    even_ref[0:halo] = jnp.swapaxes(low_ref[...], 0, 1)
    even_ref[halo + rows : 2 * halo + rows] = jnp.swapaxes(high_ref[...], 0, 1)
    for first in range(0, rows, 8):
        even_ref[halo + first : halo + first + 8] = jnp.swapaxes(
            x_ref[:, first : first + 8, :], 0, 1
        )

    def advance(src, dst, first, count):
        def several(i, carry):
            for k in range(UNROLL):
                row = first + i * UNROLL + k
                here = src[row]
                east = pltpu.roll(here, lon - 1, 1)
                west = pltpu.roll(here, 1, 1)
                c = [coeff_ref[k, pl.ds(row, 1), :] for k in range(5)]
                dst[row] = (
                    c[0] * here + c[1] * west + c[2] * east + c[3] * src[row - 1] + c[4] * src[row + 1]
                )
            return carry

        lax.fori_loop(0, (count + UNROLL - 1) // UNROLL, several, 0)

    def two(k, carry):
        first = 2 * k + 1
        count = rows + 2 * halo - 2 * first
        advance(even_ref, odd_ref, first, count)
        advance(odd_ref, even_ref, first + 1, count - 2)
        return carry

    lax.fori_loop(0, FSTEPS // 2, two, 0)
    at = 0
    for out_ref in outs:
        lanes = out_ref.shape[-1]
        out_ref[...] = even_ref[halo : halo + rows, :, at : at + lanes]
        at += lanes


def forecast(x, low, high, coeffs, start, halo_start, count, widths):
    _, rows, lon = x.shape
    group = 16 if count % 16 == 0 and start % 16 == 0 and halo_start % 16 == 0 else 8
    total = coeffs.shape[1]
    return call(
        forecast_body,
        flops=9 * FSTEPS * total * count * lon,
        moved=8 * count * rows * lon,
        grid=(count // group,),
        in_specs=[
            pl.BlockSpec((group, rows, lon), lambda i: (start // group + i, 0, 0)),
            pl.BlockSpec((group, FSTEPS, lon), lambda i: (halo_start // group + i, 0, 0)),
            pl.BlockSpec((group, FSTEPS, lon), lambda i: (halo_start // group + i, 0, 0)),
            pl.BlockSpec((5, total, lon), lambda i: (0, 0, 0)),
        ],
        out_specs=[pl.BlockSpec((rows, group, lanes), lambda i: (0, i, 0)) for lanes in widths],
        out_shape=[pltpu.HBM((rows, count, lanes), F32) for lanes in widths],
        scratch_shapes=[pltpu.VMEM((total, group, lon), F32)] * 2,
    )(x, low, high, coeffs)


def split3(value):
    top = value.astype(BF16)
    rest = value - top.astype(F32)
    middle = rest.astype(BF16)
    return top, middle, (rest - middle.astype(F32)).astype(BF16)


def observe_body(parts, cells_ref, *refs):
    chunks, out_ref = list(refs[:-1]), refs[-1]
    block_rows = chunks[0].shape[0]
    chunks = [[chunks.pop(0) for _ in range(n)] for n in parts]
    lon = sum(ref.shape[-1] for ref in chunks[0])
    obs = cells_ref.shape[-1]
    count = out_ref.shape[1]
    total = jnp.zeros((3 * count, obs), F32)
    place = lax.broadcasted_iota(jnp.int32, (lon, obs), 0)
    for row in range(block_rows):
        field = jnp.concatenate(
            [jnp.concatenate([ref[row] for ref in refs], axis=1) for refs in chunks], axis=0
        )
        chosen = jnp.where(place + row * lon == cells_ref[0], 1.0, 0.0).astype(BF16)
        total += jnp.dot(
            jnp.concatenate(split3(field), axis=0), chosen, preferred_element_type=F32
        )
    out_ref[0] = total[:count] + total[count : 2 * count] + total[2 * count :]


def observe(chunks, cells):
    rows = chunks[0][0].shape[0]
    lon = sum(part.shape[-1] for part in chunks[0])
    blocks, _, obs = cells.shape
    block_rows = rows // blocks
    count = sum(chunk[0].shape[1] for chunk in chunks)
    flat = [part for chunk in chunks for part in chunk]
    return call(
        functools.partial(observe_body, tuple(len(chunk) for chunk in chunks)),
        flops=6 * count * rows * lon * obs,
        moved=4 * count * rows * lon,
        grid=(blocks,),
        in_specs=[pl.BlockSpec((1, 1, obs), lambda k: (k, 0, 0))]
        + [pl.BlockSpec((block_rows,) + part.shape[1:], lambda k: (k, 0, 0)) for part in flat],
        out_specs=pl.BlockSpec((1, count, obs), lambda k: (k, 0, 0)),
        out_shape=jax.ShapeDtypeStruct((blocks, count, obs), F32),
    )(cells, *flat)


def mixing_body(layout, me_ref, *refs):
    banks, refs = refs[:-10], refs[-10:]
    values_ref, weights_ref, top_ref, low_ref = refs[:4]
    stacked_ref, weighted_ref, one_ref, two_ref, factor_ref, inverse_ref = refs[4:]
    size, wide = stacked_ref.shape
    sources = sum(ref.shape[0] for ref in banks)
    start = 0
    for _, count in layout:
        for step in range(sources):
            if len(banks) == 1:
                source, piece = step, banks[0].at[step]
            else:
                source, piece = me_ref[0] ^ step, banks[step].at[0]
            at = pl.multiple_of(start * sources + source * count, 8)
            stacked_ref[pl.ds(at, count), :] = piece[start : start + count, :]
        start += count
    bank = stacked_ref[...]
    mean = jnp.sum(bank, axis=0, keepdims=True) / size
    stacked = bank - mean
    innovation = values_ref[...] - mean
    weighted = stacked * weights_ref[...]
    stacked_ref[...] = stacked
    weighted_ref[...] = weighted

    def dot(a, b, contract=((1,), (0,))):
        return lax.dot_general(a, b, (contract, ((), ())), precision=HIGH, preferred_element_type=F32)

    strip = size // 2

    def halves(value):
        top = value.astype(BF16)
        return top, (value - top.astype(F32)).astype(BF16)

    def product(dst, a, b, finish=None, contract=((1,), (0,))):
        def rows_of(i, carry):
            rows = pl.ds(pl.multiple_of(i * strip, strip), strip)
            (a_top, a_low), (b_top, b_low) = halves(a[rows, :]), halves(b[...])

            def part(x, y):
                return lax.dot_general(x, y, (contract, ((), ())), preferred_element_type=F32)

            value = part(a_top, b_top) + (part(a_top, b_low) + part(a_low, b_top))
            dst[rows, :] = value if finish is None else finish(i, value)
            return carry

        lax.fori_loop(0, size // strip, rows_of, 0)

    def unit(i, shape):
        row = lax.broadcasted_iota(jnp.int32, shape, 0) + i * strip
        return jnp.where(row == lax.broadcasted_iota(jnp.int32, shape, 1), 1.0, 0.0)

    product(
        one_ref,
        weighted_ref,
        stacked_ref,
        lambda i, value: unit(i, value.shape) + value / (size - 1),
        ((1,), (1,)),
    )
    gram = one_ref[...]
    squares = jnp.sum(jnp.sum(gram * gram, axis=0, keepdims=True), axis=1, keepdims=True)
    frobenius = jnp.sqrt(squares + 1e-06)
    iterate = gram / frobenius
    one_ref[...] = iterate
    inverse_ref[...] = 1.5 * unit(0, iterate.shape) - 0.5 * iterate
    product(two_ref, one_ref, inverse_ref)
    held, spare, inverse = two_ref, one_ref, inverse_ref
    for repeat in range(1, NS_ITERS):
        product(
            factor_ref, inverse, held, lambda i, value: 1.5 * unit(i, value.shape) - 0.5 * value
        )
        if repeat < NS_ITERS - 1:
            product(spare, held, factor_ref)
            held, spare = spare, held
        product(spare, factor_ref, inverse)
        inverse, spare = spare, inverse
    inv_root = inverse[...] / jnp.sqrt(frobenius)
    spare[...] = inv_root
    innovation = jnp.broadcast_to(innovation, (8, wide))
    pull = dot(innovation, weighted_ref[...], ((1,), (1,)))
    shift = (dot(dot(pull, inv_root), inv_root) / (size - 1))[:1]
    mixing = inv_root + shift
    mixing = mixing + (1.0 - jnp.sum(mixing, axis=1, keepdims=True)) / size
    top = mixing.astype(BF16)
    top_ref[...] = top
    low_ref[...] = (mixing - top.astype(F32)).astype(BF16)


def mixing_matrix(banks, values, weights, layout):
    _, count, wide = banks[0].shape
    size = sum(bank.shape[0] for bank in banks) * count
    whole = pl.BlockSpec(memory_space=pltpu.VMEM)
    out = jax.ShapeDtypeStruct((size, size), BF16)
    return call(
        functools.partial(mixing_body, layout),
        flops=6 * 2 * 10 * size * size * size,
        moved=4 * size * (wide + size),
        in_specs=[pl.BlockSpec(memory_space=pltpu.SMEM)] + [whole] * (len(banks) + 2),
        out_shape=(out, out),
        scratch_shapes=[pltpu.VMEM((size, wide), F32)] * 2 + [pltpu.VMEM((size, size), F32)] * 4,
    )(lax.axis_index(GROUP).reshape(1), *banks, values, weights)


def analyse_body(layout, mix_top_ref, mix_low_ref, *refs):
    chunks, out_ref = refs[:-1], refs[-1]
    targets, rows, _, lanes = out_ref.shape
    field = jnp.concatenate(
        [
            jnp.concatenate(
                [ref[:, row].reshape(ref.shape[0] * ref.shape[2], lanes) for row in range(rows)], axis=1
            )
            for ref in chunks
        ],
        axis=0,
    )
    top = field.astype(BF16)
    low = (field - top.astype(F32)).astype(BF16)

    def dot(a, b):
        return jnp.dot(a, b, preferred_element_type=F32)

    mix_top = mix_top_ref[...]
    result = dot(mix_top, top) + (dot(mix_top, low) + dot(mix_low_ref[...], top))
    at = 0
    for start, count in layout:
        for target in range(targets):
            for row in range(rows):
                out_ref[target, row, start : start + count, :] = result[
                    at : at + count, row * lanes : (row + 1) * lanes
                ]
            at += count


def analyse(mix_top, mix_low, chunks, layout, lanes):
    tile = lanes if all(first % lanes == 0 for _, first in chunks) else LANES
    sources, block_rows, _, _ = chunks[0][0].shape
    count = sum(chunk.shape[2] for chunk, _ in chunks)
    size = sources * count
    step = 2 if block_rows % 2 == 0 else 1

    def spec(chunk, first):
        return pl.BlockSpec(
            (sources, step, chunk.shape[2], tile), lambda r, t: (0, r, 0, first // tile + t)
        )

    return call(
        functools.partial(analyse_body, layout),
        flops=6 * size * size * block_rows * lanes,
        moved=8 * size * block_rows * lanes,
        grid=(block_rows // step, lanes // tile),
        in_specs=[pl.BlockSpec((size, size), lambda r, t: (0, 0))] * 2
        + [spec(chunk, first) for chunk, first in chunks],
        out_specs=pl.BlockSpec((sources, step, count, tile), lambda r, t: (0, r, 0, t)),
        out_shape=pltpu.HBM((sources, block_rows, count, lanes), F32),
    )(mix_top, mix_low, *[chunk for chunk, _ in chunks])


def place_body(part_ref, *refs):
    out_ref = refs[-1]
    rows = out_ref.shape[1]
    for first in range(0, rows, 8):
        out_ref[:, first : first + 8, :] = jnp.swapaxes(part_ref[first : first + 8], 0, 1)


def place(part, whole, first, lon):
    rows, count, lanes = part.shape
    group, tile = 8, lanes if first % lanes == 0 else LANES
    out = jax.ShapeDtypeStruct((count, rows, lon), F32)
    return call(
        place_body,
        flops=0,
        moved=8 * rows * count * lanes,
        grid=(count // group, lanes // tile),
        in_specs=[pl.BlockSpec((rows, group, tile), lambda i, t: (0, i, t))]
        + ([] if whole is None else [pl.BlockSpec(memory_space=pl.ANY)]),
        out_specs=pl.BlockSpec((group, rows, tile), lambda i, t: (i, 0, first // tile + t)),
        out_shape=out,
        input_output_aliases={} if whole is None else {1: 0},
    )(*((part,) if whole is None else (part, whole)))


def place_steps_body(me_ref, *refs):
    out_ref = refs[-1]
    for step, ref in enumerate(refs[:-1]):
        if len(ref.shape) == 4:
            rows = ref.shape[1]
            at = pl.multiple_of((me_ref[0] ^ step) * rows, rows)
            out_ref[:, pl.ds(at, rows), :] = jnp.swapaxes(ref[0], 0, 1)


def place_steps(pieces, whole, first, lon):
    _, block_rows, count, lanes = pieces[0].shape
    rows, group = len(pieces) * block_rows, 8
    spec = pl.BlockSpec((1, block_rows, group, lanes), lambda i, me: (0, 0, i, 0))
    return call(
        place_steps_body,
        flops=0,
        moved=8 * rows * count * lanes,
        grid_spec=pltpu.PrefetchScalarGridSpec(
            num_scalar_prefetch=1,
            grid=(count // group,),
            in_specs=[spec] * len(pieces)
            + ([] if whole is None else [pl.BlockSpec(memory_space=pl.ANY)]),
            out_specs=pl.BlockSpec((group, rows, lanes), lambda i, me: (i, 0, first // lanes)),
        ),
        out_shape=jax.ShapeDtypeStruct((count, rows, lon), F32),
        input_output_aliases={} if whole is None else {1 + len(pieces): 0},
    )(lax.axis_index(GROUP).reshape(1), *pieces, *([] if whole is None else [whole]))


def member_chunks(count):
    if count > 24 and count % 16 == 0:
        return (count - 8, 8), (0, 16), (16, count - 24)
    return ((0, count),)


def lane_parts(lon):
    third = lon // 3
    return (2 * third, third) if lon % (3 * LANES) == 0 else (lon,)


def return_parts(lon, block_rows):
    if lon == 6 * LANES and block_rows % 8 == 0:
        third = 2 * LANES
        return (
            ((third + LANES, LANES, True), (0, third + LANES, False)),
            ((2 * third, LANES, True), (2 * third + LANES, LANES, False)),
        )
    parts = lane_parts(lon)
    return tuple(((sum(parts[:j]), lanes, False),) for j, lanes in enumerate(parts))


def gathered(row):
    size, me = lax.axis_size("members") * lax.axis_size("blk"), lax.axis_index(GROUP)
    bit = 1
    while bit < size:
        other = lax.ppermute(row, GROUP, [(i, i ^ bit) for i in range(size)])
        row = jnp.where(
            (me & bit) == 0, jnp.concatenate([row, other]), jnp.concatenate([other, row])
        )
        bit *= 2
    return row


def exchange(array):
    return lax.all_to_all(array, GROUP, split_axis=0, concat_axis=0, tiled=True)


def exchange_by_steps(array):
    size, me = array.shape[0], lax.axis_index(GROUP)
    if size > 8 or size & (size - 1):
        return [exchange(array)]
    pieces = [lax.dynamic_slice_in_dim(array, me, 1)]
    for step in range(1, size):
        piece = lax.dynamic_slice_in_dim(array, me ^ step, 1)
        pieces.append(lax.ppermute(piece, GROUP, [(i, i ^ step) for i in range(size)]))
    return pieces


def on_device(starting_states, courant_x, courant_y, diffusion, obs_index, obs_value, loc_weight):
    members, rows, lon = starting_states.shape
    blocks = lax.axis_size("members") * lax.axis_size("blk")
    block_rows = rows // blocks
    obs = obs_index.shape[-1]
    layout = member_chunks(members)
    widths = lane_parts(lon)
    halo = FSTEPS

    def edges(states):
        return shifted(states[:, rows - halo :], "lat", 1), shifted(states[:, :halo], "lat", -1)

    fields = jnp.stack([courant_x, courant_y, diffusion])
    early = layout[:2]
    head = sum(count for _, count in early)

    def ends(first):
        return jnp.concatenate(
            [starting_states[at : at + count, first : first + halo] for at, count in early]
            + [fields[:, first : first + halo]]
        )

    low = shifted(ends(rows - halo), "lat", 1)
    high = shifted(ends(0), "lat", -1)
    local = jnp.concatenate([obs_index.reshape(1, obs).astype(F32), obs_value.reshape(1, obs)])
    everyone = gathered(local[None])
    spare = jnp.zeros((3, UNROLL + 8, lon), F32)
    fields = jnp.concatenate([low[head:], fields, high[head:], spare], axis=1)
    across, along, spread = 0.5 * fields[0], 0.5 * fields[1], fields[2]
    coeffs = jnp.stack(
        [1.0 - 4.0 * spread, across + spread, spread - across, along + spread, spread - along]
    )

    states = []
    halos, at = (low[:head], high[:head]), 0
    for i, (start, count) in enumerate(layout):
        parts = widths if i == len(layout) - 1 else (lon,)
        if i == 2:
            halos, at = halos_rest, 0
        state = forecast(starting_states, *halos, coeffs, start, at, count, parts)
        at += count
        states.append(state)
        if i == 0 and len(layout) > 2:
            later, _ = lax.optimization_barrier((starting_states, state[0]))
            halos_rest = edges(later[layout[2][0] : layout[2][0] + layout[2][1]])
    received = []
    for i, state in enumerate(states):
        received.append([])
        for part in state:
            received[i].append(exchange(part.reshape(blocks, block_rows, *part.shape[1:])))

    cells = everyone[:, :1].astype(jnp.int32)
    own = observe(states, cells)
    zero = jnp.zeros((1,) + own.shape[1:], F32)
    triple = jnp.concatenate(
        [jnp.concatenate([zero, own[:-1]]), own, jnp.concatenate([own[1:], zero])], axis=2
    )
    banks = exchange_by_steps(triple)
    zero = jnp.zeros((1, obs), F32)
    values = jnp.concatenate([zero, everyone[:, 1], zero])
    values = lax.dynamic_slice_in_dim(values, lax.axis_index(GROUP), 3).reshape(1, 3 * obs)
    mix_top, mix_low = mixing_matrix(banks, values, loc_weight.reshape(1, 3 * obs), layout)

    result = None
    for j, pieces in enumerate(return_parts(lon, block_rows)):
        base = sum(widths[:j])
        for first, lanes, stepwise in pieces:
            chunks = [
                (chunk[0], first) if len(chunk) == 1 else (chunk[j], first - base) for chunk in received
            ]
            part = analyse(mix_top, mix_low, chunks, layout, lanes)
            part = exchange_by_steps(part) if stepwise else exchange(part)
            if stepwise and len(part) > 1:
                result = place_steps(part, result, first, lon)
            else:
                part = part[0] if stepwise else part
                result = place(part.reshape(rows, members, lanes), result, first, lon)
    return result


def solution(mesh):
    in_specs = (
        P(GROUP, "lat", None),
        P("lat", None),
        P("lat", None),
        P("lat", None),
        P("lat", GROUP, None),
        P("lat", GROUP, None),
        P("lat", GROUP, None, None),
    )

    return jax.shard_map(
        on_device, mesh=mesh, in_specs=in_specs, out_specs=P(GROUP, "lat", None), check_vma=False
    )
```

```python
import functools
import jax
import jax.numpy as jnp
from jax import lax
from jax.experimental import pallas as pl
from jax.experimental.pallas import tpu as pltpu
from jax.sharding import PartitionSpec as P


FSTEPS = 8
NS_ITERS = 4
LANES = 128

HIGH = lax.Precision.HIGHEST
GROUP = ("members", "blk")
F32 = jnp.float32
BF16 = jnp.bfloat16


def call(kernel, flops, moved, **kwargs):
    return pl.pallas_call(
        kernel,
        compiler_params=pltpu.CompilerParams(vmem_limit_bytes=48 << 20),
        cost_estimate=pl.CostEstimate(flops=flops, bytes_accessed=moved, transcendentals=0),
        **kwargs,
    )


def shifted(array, axis, by):
    size = lax.axis_size(axis)
    pairs = [(i, i + by) for i in range(size) if 0 <= i + by < size]
    return lax.ppermute(array, axis, pairs)


UNROLL = 16


def forecast_body(x_ref, low_ref, high_ref, coeff_ref, *refs):
    outs, (even_ref, odd_ref, wide_ref) = refs[:-3], refs[-3:]
    group, rows, lon = x_ref.shape
    halo = FSTEPS

    @pl.when(pl.program_id(0) == 0)
    def _():
        def widen(row, carry):
            for k in range(5):
                wide_ref[k, row] = jnp.broadcast_to(coeff_ref[k, pl.ds(row, 1), :], (8, lon))
            return carry

        lax.fori_loop(0, rows + 2 * halo, widen, 0, unroll=4)

    even_ref[0:halo] = jnp.swapaxes(low_ref[...], 0, 1)
    even_ref[halo + rows : 2 * halo + rows] = jnp.swapaxes(high_ref[...], 0, 1)
    for first in range(0, rows, 8):
        even_ref[halo + first : halo + first + 8] = jnp.swapaxes(
            x_ref[:, first : first + 8, :], 0, 1
        )

    def advance(src, dst, first, count):
        def several(i, carry):
            for k in range(UNROLL):
                row = first + i * UNROLL + k
                here = src[row]
                east = pltpu.roll(here, lon - 1, 1)
                west = pltpu.roll(here, 1, 1)
                c = [jnp.concatenate([wide_ref[k, row]] * (group // 8)) for k in range(5)]
                dst[row] = (
                    c[0] * here + c[1] * west + c[2] * east + c[3] * src[row - 1] + c[4] * src[row + 1]
                )
            return carry

        lax.fori_loop(0, (count + UNROLL - 1) // UNROLL, several, 0)

    def two(k, carry):
        first = 2 * k + 1
        count = rows + 2 * halo - 2 * first
        advance(even_ref, odd_ref, first, count)
        advance(odd_ref, even_ref, first + 1, count - 2)
        return carry

    lax.fori_loop(0, FSTEPS // 2, two, 0)
    at = 0
    for out_ref in outs:
        lanes = out_ref.shape[-1]
        out_ref[...] = even_ref[halo : halo + rows, :, at : at + lanes]
        at += lanes


def forecast(x, low, high, coeffs, start, halo_start, count, widths):
    _, rows, lon = x.shape
    group = 16 if count % 16 == 0 and start % 16 == 0 and halo_start % 16 == 0 else 8
    total = coeffs.shape[1]
    return call(
        forecast_body,
        flops=9 * FSTEPS * total * count * lon,
        moved=8 * count * rows * lon,
        grid=(count // group,),
        in_specs=[
            pl.BlockSpec((group, rows, lon), lambda i: (start // group + i, 0, 0)),
            pl.BlockSpec((group, FSTEPS, lon), lambda i: (halo_start // group + i, 0, 0)),
            pl.BlockSpec((group, FSTEPS, lon), lambda i: (halo_start // group + i, 0, 0)),
            pl.BlockSpec((5, total, lon), lambda i: (0, 0, 0)),
        ],
        out_specs=[pl.BlockSpec((rows, group, lanes), lambda i: (0, i, 0)) for lanes in widths],
        out_shape=[pltpu.HBM((rows, count, lanes), F32) for lanes in widths],
        scratch_shapes=[pltpu.VMEM((total, group, lon), F32)] * 2
        + [pltpu.VMEM((5, total, 8, lon), F32)],
    )(x, low, high, coeffs)


def split3(value):
    top = value.astype(BF16)
    rest = value - top.astype(F32)
    middle = rest.astype(BF16)
    return top, middle, (rest - middle.astype(F32)).astype(BF16)


def observe_body(parts, cells_ref, *refs):
    chunks, out_ref = list(refs[:-1]), refs[-1]
    block_rows = chunks[0].shape[0]
    chunks = [[chunks.pop(0) for _ in range(n)] for n in parts]
    lon = sum(ref.shape[-1] for ref in chunks[0])
    obs = cells_ref.shape[-1]
    count = out_ref.shape[1]
    total = jnp.zeros((3 * count, obs), F32)
    place = lax.broadcasted_iota(jnp.int32, (lon, obs), 0)
    for row in range(block_rows):
        field = jnp.concatenate(
            [jnp.concatenate([ref[row] for ref in refs], axis=1) for refs in chunks], axis=0
        )
        chosen = jnp.where(place + row * lon == cells_ref[0], 1.0, 0.0).astype(BF16)
        total += jnp.dot(
            jnp.concatenate(split3(field), axis=0), chosen, preferred_element_type=F32
        )
    out_ref[0] = total[:count] + total[count : 2 * count] + total[2 * count :]


def observe(chunks, cells):
    rows = chunks[0][0].shape[0]
    lon = sum(part.shape[-1] for part in chunks[0])
    blocks, _, obs = cells.shape
    block_rows = rows // blocks
    count = sum(chunk[0].shape[1] for chunk in chunks)
    flat = [part for chunk in chunks for part in chunk]
    return call(
        functools.partial(observe_body, tuple(len(chunk) for chunk in chunks)),
        flops=6 * count * rows * lon * obs,
        moved=4 * count * rows * lon,
        grid=(blocks,),
        in_specs=[pl.BlockSpec((1, 1, obs), lambda k: (k, 0, 0))]
        + [pl.BlockSpec((block_rows,) + part.shape[1:], lambda k: (k, 0, 0)) for part in flat],
        out_specs=pl.BlockSpec((1, count, obs), lambda k: (k, 0, 0)),
        out_shape=jax.ShapeDtypeStruct((blocks, count, obs), F32),
    )(cells, *flat)


def mixing_body(layout, me_ref, *refs):
    banks, refs = refs[:-10], refs[-10:]
    values_ref, weights_ref, top_ref, low_ref = refs[:4]
    stacked_ref, weighted_ref, one_ref, two_ref, factor_ref, inverse_ref = refs[4:]
    size, wide = stacked_ref.shape
    sources = sum(ref.shape[0] for ref in banks)
    start = 0
    for _, count in layout:
        for step in range(sources):
            if len(banks) == 1:
                source, piece = step, banks[0].at[step]
            else:
                source, piece = me_ref[0] ^ step, banks[step].at[0]
            at = pl.multiple_of(start * sources + source * count, 8)
            stacked_ref[pl.ds(at, count), :] = piece[start : start + count, :]
        start += count
    bank = stacked_ref[...]
    mean = jnp.sum(bank, axis=0, keepdims=True) / size
    stacked = bank - mean
    innovation = values_ref[...] - mean
    weighted = stacked * weights_ref[...]
    stacked_ref[...] = stacked
    weighted_ref[...] = weighted

    def dot(a, b, contract=((1,), (0,))):
        return lax.dot_general(a, b, (contract, ((), ())), precision=HIGH, preferred_element_type=F32)

    strip = size // 2

    def halves(value):
        top = value.astype(BF16)
        return top, (value - top.astype(F32)).astype(BF16)

    def product(dst, a, b, finish=None, contract=((1,), (0,))):
        def rows_of(i, carry):
            rows = pl.ds(pl.multiple_of(i * strip, strip), strip)
            (a_top, a_low), (b_top, b_low) = halves(a[rows, :]), halves(b[...])

            def part(x, y):
                return lax.dot_general(x, y, (contract, ((), ())), preferred_element_type=F32)

            value = part(a_top, b_top) + (part(a_top, b_low) + part(a_low, b_top))
            dst[rows, :] = value if finish is None else finish(i, value)
            return carry

        lax.fori_loop(0, size // strip, rows_of, 0)

    def unit(i, shape):
        row = lax.broadcasted_iota(jnp.int32, shape, 0) + i * strip
        return jnp.where(row == lax.broadcasted_iota(jnp.int32, shape, 1), 1.0, 0.0)

    product(
        one_ref,
        weighted_ref,
        stacked_ref,
        lambda i, value: unit(i, value.shape) + value / (size - 1),
        ((1,), (1,)),
    )
    gram = one_ref[...]
    squares = jnp.sum(jnp.sum(gram * gram, axis=0, keepdims=True), axis=1, keepdims=True)
    frobenius = jnp.sqrt(squares + 1e-06)
    iterate = gram / frobenius
    one_ref[...] = iterate
    inverse_ref[...] = 1.5 * unit(0, iterate.shape) - 0.5 * iterate
    product(two_ref, one_ref, inverse_ref)
    held, spare, inverse = two_ref, one_ref, inverse_ref
    for repeat in range(1, NS_ITERS):
        product(
            factor_ref, inverse, held, lambda i, value: 1.5 * unit(i, value.shape) - 0.5 * value
        )
        if repeat < NS_ITERS - 1:
            product(spare, held, factor_ref)
            held, spare = spare, held
        product(spare, factor_ref, inverse)
        inverse, spare = spare, inverse
    inv_root = inverse[...] / jnp.sqrt(frobenius)
    spare[...] = inv_root
    innovation = jnp.broadcast_to(innovation, (8, wide))
    pull = dot(innovation, weighted_ref[...], ((1,), (1,)))
    shift = (dot(dot(pull, inv_root), inv_root) / (size - 1))[:1]
    mixing = inv_root + shift
    mixing = mixing + (1.0 - jnp.sum(mixing, axis=1, keepdims=True)) / size
    top = mixing.astype(BF16)
    top_ref[...] = top
    low_ref[...] = (mixing - top.astype(F32)).astype(BF16)


def mixing_matrix(banks, values, weights, layout):
    _, count, wide = banks[0].shape
    size = sum(bank.shape[0] for bank in banks) * count
    whole = pl.BlockSpec(memory_space=pltpu.VMEM)
    out = jax.ShapeDtypeStruct((size, size), BF16)
    return call(
        functools.partial(mixing_body, layout),
        flops=6 * 2 * 10 * size * size * size,
        moved=4 * size * (wide + size),
        in_specs=[pl.BlockSpec(memory_space=pltpu.SMEM)] + [whole] * (len(banks) + 2),
        out_shape=(out, out),
        scratch_shapes=[pltpu.VMEM((size, wide), F32)] * 2 + [pltpu.VMEM((size, size), F32)] * 4,
    )(lax.axis_index(GROUP).reshape(1), *banks, values, weights)


def analyse_body(layout, mix_top_ref, mix_low_ref, *refs):
    chunks, out_ref = refs[:-1], refs[-1]
    targets, rows, _, lanes = out_ref.shape
    field = jnp.concatenate(
        [
            jnp.concatenate(
                [ref[:, row].reshape(ref.shape[0] * ref.shape[2], lanes) for row in range(rows)], axis=1
            )
            for ref in chunks
        ],
        axis=0,
    )
    top = field.astype(BF16)
    low = (field - top.astype(F32)).astype(BF16)

    def dot(a, b):
        return jnp.dot(a, b, preferred_element_type=F32)

    mix_top = mix_top_ref[...]
    result = dot(mix_top, top) + (dot(mix_top, low) + dot(mix_low_ref[...], top))
    at = 0
    for start, count in layout:
        for target in range(targets):
            for row in range(rows):
                out_ref[target, row, start : start + count, :] = result[
                    at : at + count, row * lanes : (row + 1) * lanes
                ]
            at += count


def analyse(mix_top, mix_low, chunks, layout, lanes):
    tile = lanes if all(first % lanes == 0 for _, first in chunks) else LANES
    sources, block_rows, _, _ = chunks[0][0].shape
    count = sum(chunk.shape[2] for chunk, _ in chunks)
    size = sources * count
    step = 2 if block_rows % 2 == 0 else 1

    def spec(chunk, first):
        return pl.BlockSpec(
            (sources, step, chunk.shape[2], tile), lambda r, t: (0, r, 0, first // tile + t)
        )

    return call(
        functools.partial(analyse_body, layout),
        flops=6 * size * size * block_rows * lanes,
        moved=8 * size * block_rows * lanes,
        grid=(block_rows // step, lanes // tile),
        in_specs=[pl.BlockSpec((size, size), lambda r, t: (0, 0))] * 2
        + [spec(chunk, first) for chunk, first in chunks],
        out_specs=pl.BlockSpec((sources, step, count, tile), lambda r, t: (0, r, 0, t)),
        out_shape=pltpu.HBM((sources, block_rows, count, lanes), F32),
    )(mix_top, mix_low, *[chunk for chunk, _ in chunks])


def place_body(part_ref, *refs):
    out_ref = refs[-1]
    rows = out_ref.shape[1]
    for first in range(0, rows, 8):
        out_ref[:, first : first + 8, :] = jnp.swapaxes(part_ref[first : first + 8], 0, 1)


def place(part, whole, first, lon):
    rows, count, lanes = part.shape
    group, tile = 8, lanes if first % lanes == 0 else LANES
    out = jax.ShapeDtypeStruct((count, rows, lon), F32)
    return call(
        place_body,
        flops=0,
        moved=8 * rows * count * lanes,
        grid=(count // group, lanes // tile),
        in_specs=[pl.BlockSpec((rows, group, tile), lambda i, t: (0, i, t))]
        + ([] if whole is None else [pl.BlockSpec(memory_space=pl.ANY)]),
        out_specs=pl.BlockSpec((group, rows, tile), lambda i, t: (i, 0, first // tile + t)),
        out_shape=out,
        input_output_aliases={} if whole is None else {1: 0},
    )(*((part,) if whole is None else (part, whole)))


def place_steps_body(me_ref, *refs):
    out_ref = refs[-1]
    for step, ref in enumerate(refs[:-1]):
        if len(ref.shape) == 4:
            rows = ref.shape[1]
            at = pl.multiple_of((me_ref[0] ^ step) * rows, rows)
            out_ref[:, pl.ds(at, rows), :] = jnp.swapaxes(ref[0], 0, 1)


def place_steps(pieces, whole, first, lon):
    _, block_rows, count, lanes = pieces[0].shape
    rows, group = len(pieces) * block_rows, 8
    spec = pl.BlockSpec((1, block_rows, group, lanes), lambda i, me: (0, 0, i, 0))
    return call(
        place_steps_body,
        flops=0,
        moved=8 * rows * count * lanes,
        grid_spec=pltpu.PrefetchScalarGridSpec(
            num_scalar_prefetch=1,
            grid=(count // group,),
            in_specs=[spec] * len(pieces)
            + ([] if whole is None else [pl.BlockSpec(memory_space=pl.ANY)]),
            out_specs=pl.BlockSpec((group, rows, lanes), lambda i, me: (i, 0, first // lanes)),
        ),
        out_shape=jax.ShapeDtypeStruct((count, rows, lon), F32),
        input_output_aliases={} if whole is None else {1 + len(pieces): 0},
    )(lax.axis_index(GROUP).reshape(1), *pieces, *([] if whole is None else [whole]))


def member_chunks(count):
    if count > 24 and count % 16 == 0:
        return (count - 8, 8), (0, 16), (16, count - 24)
    return ((0, count),)


def lane_parts(lon):
    third = lon // 3
    return (2 * third, third) if lon % (3 * LANES) == 0 else (lon,)


def return_parts(lon, block_rows):
    if lon == 6 * LANES and block_rows % 8 == 0:
        third = 2 * LANES
        return (
            ((third + LANES, LANES, True), (0, third + LANES, False)),
            ((2 * third, LANES, True), (2 * third + LANES, LANES, False)),
        )
    parts = lane_parts(lon)
    return tuple(((sum(parts[:j]), lanes, False),) for j, lanes in enumerate(parts))


def gathered(row):
    size, me = lax.axis_size("members") * lax.axis_size("blk"), lax.axis_index(GROUP)
    bit = 1
    while bit < size:
        other = lax.ppermute(row, GROUP, [(i, i ^ bit) for i in range(size)])
        row = jnp.where(
            (me & bit) == 0, jnp.concatenate([row, other]), jnp.concatenate([other, row])
        )
        bit *= 2
    return row


def exchange(array):
    return lax.all_to_all(array, GROUP, split_axis=0, concat_axis=0, tiled=True)


def exchange_by_steps(array):
    size, me = array.shape[0], lax.axis_index(GROUP)
    if size > 8 or size & (size - 1):
        return [exchange(array)]
    pieces = [lax.dynamic_slice_in_dim(array, me, 1)]
    for step in range(1, size):
        piece = lax.dynamic_slice_in_dim(array, me ^ step, 1)
        pieces.append(lax.ppermute(piece, GROUP, [(i, i ^ step) for i in range(size)]))
    return pieces


def on_device(starting_states, courant_x, courant_y, diffusion, obs_index, obs_value, loc_weight):
    members, rows, lon = starting_states.shape
    blocks = lax.axis_size("members") * lax.axis_size("blk")
    block_rows = rows // blocks
    obs = obs_index.shape[-1]
    layout = member_chunks(members)
    widths = lane_parts(lon)
    halo = FSTEPS

    def edges(states):
        return shifted(states[:, rows - halo :], "lat", 1), shifted(states[:, :halo], "lat", -1)

    fields = jnp.stack([courant_x, courant_y, diffusion])
    early = layout[:2]
    head = sum(count for _, count in early)

    def ends(first):
        return jnp.concatenate(
            [starting_states[at : at + count, first : first + halo] for at, count in early]
            + [fields[:, first : first + halo]]
        )

    low = shifted(ends(rows - halo), "lat", 1)
    high = shifted(ends(0), "lat", -1)
    local = jnp.concatenate([obs_index.reshape(1, obs).astype(F32), obs_value.reshape(1, obs)])
    everyone = gathered(local[None])
    spare = jnp.zeros((3, UNROLL + 8, lon), F32)
    fields = jnp.concatenate([low[head:], fields, high[head:], spare], axis=1)
    across, along, spread = 0.5 * fields[0], 0.5 * fields[1], fields[2]
    coeffs = jnp.stack(
        [1.0 - 4.0 * spread, across + spread, spread - across, along + spread, spread - along]
    )

    states = []
    halos, at = (low[:head], high[:head]), 0
    for i, (start, count) in enumerate(layout):
        parts = widths if i == len(layout) - 1 else (lon,)
        if i == 2:
            halos, at = halos_rest, 0
        state = forecast(starting_states, *halos, coeffs, start, at, count, parts)
        at += count
        states.append(state)
        if i == 1 and len(layout) > 2:
            later, _ = lax.optimization_barrier((starting_states, state[0]))
            halos_rest = edges(later[layout[2][0] : layout[2][0] + layout[2][1]])
    received = []
    for i, state in enumerate(states):
        received.append([])
        for part in state:
            received[i].append(exchange(part.reshape(blocks, block_rows, *part.shape[1:])))

    cells = everyone[:, :1].astype(jnp.int32)
    own = observe(states, cells)
    zero = jnp.zeros((1,) + own.shape[1:], F32)
    triple = jnp.concatenate(
        [jnp.concatenate([zero, own[:-1]]), own, jnp.concatenate([own[1:], zero])], axis=2
    )
    banks = exchange_by_steps(triple)
    zero = jnp.zeros((1, obs), F32)
    values = jnp.concatenate([zero, everyone[:, 1], zero])
    values = lax.dynamic_slice_in_dim(values, lax.axis_index(GROUP), 3).reshape(1, 3 * obs)
    mix_top, mix_low = mixing_matrix(banks, values, loc_weight.reshape(1, 3 * obs), layout)

    result = None
    for j, pieces in enumerate(return_parts(lon, block_rows)):
        base = sum(widths[:j])
        for first, lanes, stepwise in pieces:
            chunks = [
                (chunk[0], first) if len(chunk) == 1 else (chunk[j], first - base) for chunk in received
            ]
            part = analyse(mix_top, mix_low, chunks, layout, lanes)
            part = exchange_by_steps(part) if stepwise else exchange(part)
            if stepwise and len(part) > 1:
                result = place_steps(part, result, first, lon)
            else:
                part = part[0] if stepwise else part
                result = place(part.reshape(rows, members, lanes), result, first, lon)
    return result


def solution(mesh):
    in_specs = (
        P(GROUP, "lat", None),
        P("lat", None),
        P("lat", None),
        P("lat", None),
        P("lat", GROUP, None),
        P("lat", GROUP, None),
        P("lat", GROUP, None, None),
    )

    return jax.shard_map(
        on_device, mesh=mesh, in_specs=in_specs, out_specs=P(GROUP, "lat", None), check_vma=False
    )
```
